32 devices in a mesh: fsdp: 8 (over z, x), tp: 4 (over y, core).
Axes of the slice: x: 2, y: 2, z: 4, core: 2. Of those that a mesh axis runs over, the one named last changes fastest.
Arguments:
- tokens: bfloat16 [128, 4096], P('fsdp', 'tp'), may hold values from -6 to 6
- route_logits: bfloat16 [128, 2], P('fsdp'), may hold values from -6 to 6
- route_ids: int32 [128, 2], P('fsdp'), may hold values from 0 to 7, all different within a row; in each aligned block of 128 rows (0 to 127, 128 to 255, ...) at most 64 rows name the same one
- gate_codes: bfloat16 [8, 14336, 4096], P(None, 'fsdp', 'tp'), may hold values from -4 to 4
- gate_scales: float32 [8, 14336, 32], P(None, 'fsdp', 'tp'), may hold values from 0.008 to 0.03
- up_codes: bfloat16 [8, 14336, 4096], P(None, 'fsdp', 'tp'), may hold values from -4 to 4
- up_scales: float32 [8, 14336, 32], P(None, 'fsdp', 'tp'), may hold values from 0.008 to 0.03
- down_codes: bfloat16 [8, 14336, 4096], P(None, 'fsdp', 'tp'), may hold values from -4 to 4
- down_scales: float32 [8, 14336, 32], P(None, 'fsdp', 'tp'), may hold values from 0.004 to 0.016
Outputs:
- mixed: bfloat16 [128, 4096], P('fsdp', 'tp')
The draws below stay inside these ranges and needn't reach their ends.
Inputs may be any that keep to these rules, and one draw needn't show every extreme that they name: `route_ids`: each row names two different experts; over all 128 rows no expert is named more than 64 times, a bound that some block reaches.
All inputs are finite; a program needn't handle non-finite values.
Results may differ from the reference program's by a relative error of at most 0.011.
Values may be sent and summed in bfloat16 or wider, within the bound.
No kernel may reach another device: no remote copies, remote signals or barrier semaphores. Data moves between devices by JAX's collectives and lax.ppermute only.
A program may use at most 320 MiB of HBM per device.

```python
import math
import jax
import jax.numpy as jnp
import numpy as np
from jax import lax

D = 4096
FF = 14336
EXPERTS = 8
TOP = 2
QBLOCK = 128
TOKENS = 128
CAP = 64


def level_of(rng, extent, shards, low, largest):
    level, own = 1.0, jax.random.fold_in(rng, 6)
    for position, parts in shards:
        draws = jnp.exp(jax.random.uniform(jax.random.fold_in(own, position), (parts,), jnp.float32, low / len(shards), largest / len(shards)))
        level = level * jnp.repeat(draws, extent[position] // parts).reshape([-1 if axis == position else 1 for axis in range(len(extent))])
    return level


def assign_block(own_key, own, number, rows, amount, top, bound, lean):
    sequence = jax.random.permutation(own_key, amount)
    heavy_load, usual = load_shares(amount, rows * top, bound, lean, True), load_shares(amount, rows * top, bound, lean, False)
    places = jnp.arange(amount)

    def named(tallies, turn):
        used = int((tallies > 0).sum())
        fixed = max(1, used // 4)
        shifted = fixed + (places - fixed + turn * (used - fixed)) % max(1, amount - fixed)
        return jnp.zeros((amount,), jnp.int32).at[sequence[jnp.where(places < fixed, places, shifted)]].set(jnp.asarray(tallies, jnp.int32))

    tallies = jnp.where(number % 4 == 0, named(heavy_load, number // 4), named(usual, number - number // 4 - 1))
    mixed = jax.random.permutation(jax.random.fold_in(own, 3), amount)
    donor, sink = mixed[0:amount // 2 * 2:2], mixed[1:amount // 2 * 2:2]
    room = jnp.minimum(tallies[donor] - 1, bound - tallies[sink]) // 2
    room = jnp.where((donor == sequence[0]) | (sink == sequence[0]) | (tallies[sink] == 0), 0, jnp.maximum(room, 0))
    shifted = jax.random.randint(jax.random.fold_in(own, 4), (amount // 2,), 0, 1 << 20) % (room + 1)
    tallies = tallies.at[donor].add(-shifted).at[sink].add(shifted)
    labels = jnp.searchsorted(jnp.cumsum(tallies), jnp.arange(rows * top), side="right").astype(jnp.int32)
    grid = labels.reshape(top, rows).T
    grid = grid[jax.random.permutation(jax.random.fold_in(own, 1), rows)]
    turn = jax.random.randint(jax.random.fold_in(own, 2), (rows, 1), 0, top)
    return jnp.take_along_axis(grid, (jnp.arange(top)[None, :] + turn) % top, axis=1)


def load_shares(number_of, total, limit, skew, full):
    portions = [(1 << 20) // math.isqrt(rank ** skew) + 1 for rank in range(1, number_of + 1)]
    largest = limit if full else min(limit, max(-(-total // number_of), total * portions[0] // sum(portions)))
    least = 1 if total - largest >= number_of - 1 else 0
    given, rest = [largest] + [least] * (number_of - 1), total - largest - least * (number_of - 1)
    while rest > 0:
        free = [i for i in range(1, number_of) if given[i] < largest] or [i for i in range(1, number_of) if given[i] < limit]
        pool, budget = sum([portions[i] for i in free]), rest
        for i in free:
            more = min(limit - given[i], max(1, budget * portions[i] // pool), rest)
            given[i] = given[i] + more
            rest = rest - more
    return np.array(given)


def centred(stream_key, dims, spread, bound, shards=(), kind=jnp.bfloat16):
    array = spread * jax.random.normal(stream_key, dims, jnp.float32)
    if shards:
        array = array * level_of(stream_key, dims, shards, -0.22, 0.18)
    return jnp.clip(array, -bound, bound).astype(kind)


def setup_inputs(seed: int = 0) -> dict:
    streams_of = jax.random.split(jax.random.key(seed), 10)
    tokens = centred(streams_of[0], (TOKENS, D), 1.0, 6.0, ((0, 8), (1, 4)))
    route_logits = centred(streams_of[1], (TOKENS, TOP), 1.5, 6.0, ((0, 8),))
    route_ids_keys = jax.random.split(jax.random.fold_in(streams_of[2], 1), TOKENS // TOKENS)
    route_ids_turns = jax.random.permutation(jax.random.fold_in(streams_of[2], 3), TOKENS // TOKENS)
    route_ids = jax.vmap(lambda own, number: assign_block(jax.random.fold_in(streams_of[2], 2), own, number, TOKENS, EXPERTS, TOP, CAP, 2))(route_ids_keys, route_ids_turns).reshape((TOKENS, TOP))
    gate_codes = centred(streams_of[3], (EXPERTS, FF, D), 1.0, 4.0, ((1, 8), (2, 4)))
    gate_scales = jnp.clip(jnp.exp(math.log(0.03) - 1.3217558 * jax.random.uniform(streams_of[4], (EXPERTS, FF, D // QBLOCK), jnp.float32) ** level_of(streams_of[4], (EXPERTS, FF, D // QBLOCK), ((1, 8), (2, 4)), -0.2, 0.2)), 0.008, 0.03)
    up_codes = centred(streams_of[5], (EXPERTS, FF, D), 1.0, 4.0, ((1, 8), (2, 4)))
    up_scales = jnp.clip(jnp.exp(math.log(0.03) - 1.3217558 * jax.random.uniform(streams_of[6], (EXPERTS, FF, D // QBLOCK), jnp.float32) ** level_of(streams_of[6], (EXPERTS, FF, D // QBLOCK), ((1, 8), (2, 4)), -0.2, 0.2)), 0.008, 0.03)
    down_codes = centred(streams_of[7], (EXPERTS, FF, D), 1.0, 4.0, ((1, 8), (2, 4)))
    down_scales = jnp.clip(jnp.exp(math.log(0.016) - 1.3862944 * jax.random.uniform(streams_of[8], (EXPERTS, FF, D // QBLOCK), jnp.float32) ** level_of(streams_of[8], (EXPERTS, FF, D // QBLOCK), ((1, 8), (2, 4)), -0.2, 0.2)), 0.004, 0.016)
    return dict(tokens=tokens, route_logits=route_logits, route_ids=route_ids, gate_codes=gate_codes, gate_scales=gate_scales, up_codes=up_codes, up_scales=up_scales, down_codes=down_codes, down_scales=down_scales)


def dispatch(route_ids, experts, capacity):
    flat_ids = route_ids.reshape(-1).astype(jnp.int32)
    one_hot = (flat_ids[:, None] == jnp.arange(experts, dtype=jnp.int32)[None, :]).astype(jnp.int32)
    earlier = (jnp.cumsum(one_hot, axis=0) - one_hot).astype(jnp.int32)
    slot_rank = jnp.sum(earlier * one_hot, axis=1).astype(jnp.int32)
    return (flat_ids * capacity + slot_rank).astype(jnp.int32)


def expand_cols(codes, scales):
    leading, row_count, col_count = codes.shape
    blocks = scales.shape[2]
    grouped = codes.astype(jnp.float32).reshape(leading, row_count, blocks, col_count // blocks)
    grouped = grouped * scales[:, :, :, None]
    return grouped.reshape(leading, row_count, col_count).astype(jnp.bfloat16)


def reference(tokens, route_logits, route_ids, gate_codes, gate_scales, up_codes, up_scales, down_codes, down_scales):
    places = dispatch(route_ids, EXPERTS, CAP)
    repeated = jnp.repeat(tokens, 2, axis=0)
    slots = jnp.zeros((EXPERTS * CAP, D), jnp.bfloat16).at[places].set(repeated).reshape(EXPERTS, CAP, D)

    def one_expert(pieces):
        rows_in, gate_code, gate_scale, up_code, up_scale, down_code, down_scale = pieces
        gate_w = expand_cols(gate_code[None], gate_scale[None])[0]
        up_w = expand_cols(up_code[None], up_scale[None])[0]
        down_w = expand_cols(down_code[None], down_scale[None])[0]
        contract = (((1,), (1,)), ((), ()))
        gate_sum = lax.dot_general(rows_in, gate_w, contract, preferred_element_type=jnp.float32)
        up_sum = lax.dot_general(rows_in, up_w, contract, preferred_element_type=jnp.float32)
        hidden = (jax.nn.silu(gate_sum) * up_sum).astype(jnp.bfloat16)
        return jnp.dot(hidden, down_w, preferred_element_type=jnp.float32)

    outputs = lax.map(one_expert, (slots, gate_codes, gate_scales, up_codes, up_scales, down_codes, down_scales))
    routed = outputs.reshape(EXPERTS * CAP, D)[places].reshape(TOKENS, 2, D)
    logits = route_logits.astype(jnp.float32)
    first_w = jax.nn.sigmoid(logits[:, 0] - logits[:, 1])
    second_w = jax.nn.sigmoid(logits[:, 1] - logits[:, 0])
    mixed = routed[:, 0] * first_w[:, None] + routed[:, 1] * second_w[:, None]
    return mixed.astype(jnp.bfloat16)
```

```python
import functools

import jax
import jax.numpy as jnp
from jax import lax
from jax.experimental import pallas as pl
from jax.experimental.pallas import tpu as pltpu
from jax.sharding import PartitionSpec as P

F32, BF16 = jnp.float32, jnp.bfloat16


def exchange(value, axis, mask, size):
    return lax.ppermute(value, axis, [(i, i ^ mask) for i in range(size)])


def gate_up_kernel(x_ref, ids_ref, gc_ref, gs_ref, uc_ref, us_ref, mine_ref, theirs_ref, acc_ref):
    experts, width, feats = gc_ref.shape
    blocks = gs_ref.shape[1]
    qb = feats // blocks
    for e in range(experts):
        hit_mine = ids_ref[:, 0:1] == e
        hit_theirs = ids_ref[:, 1:2] == e
        for m, (c_ref, s_ref) in enumerate(((gc_ref, gs_ref), (uc_ref, us_ref))):
            total = None
            for b in range(blocks):
                cols = slice(b * qb, (b + 1) * qb)
                part = lax.dot_general(
                    x_ref[:, cols], c_ref[e, :, cols], (((1,), (1,)), ((), ())), preferred_element_type=F32
                )
                part = part * s_ref[e, b : b + 1, :]
                total = part if total is None else total + part
            acc_ref[m, 0] = jnp.where(hit_mine, total, acc_ref[m, 0])
            acc_ref[m, 1] = jnp.where(hit_theirs, total, acc_ref[m, 1])
    mine_ref[...] = acc_ref[:, 0].astype(BF16)
    theirs_ref[...] = acc_ref[:, 1].astype(BF16)


def gate_up(x, ids, gc, gs, uc, us, first, count, width):
    experts, _, feats = gc.shape
    blocks, rows = gs.shape[1], x.shape[0]
    w_spec = pl.BlockSpec((experts, width, feats), lambda i: (0, first + i, 0))
    s_spec = pl.BlockSpec((experts, blocks, width), lambda i: (0, 0, first + i))
    o_spec = pl.BlockSpec((2, rows, width), lambda i: (0, 0, i))
    out = jax.ShapeDtypeStruct((2, rows, count * width), BF16)
    moved = 2 * experts * count * width * feats * 2
    return pl.pallas_call(
        gate_up_kernel,
        out_shape=(out, out),
        grid=(count,),
        in_specs=[
            pl.BlockSpec(x.shape, lambda i: (0, 0)),
            pl.BlockSpec(ids.shape, lambda i: (0, 0)),
            w_spec,
            s_spec,
            w_spec,
            s_spec,
        ],
        out_specs=(o_spec, o_spec),
        scratch_shapes=[pltpu.VMEM((2, 2, rows, width), F32)],
        cost_estimate=pl.CostEstimate(flops=moved * rows, transcendentals=0, bytes_accessed=moved),
        name="gate_up",
    )(x, ids, gc, gs, uc, us)


def down_kernel(mine_ref, theirs_ref, ids_ref, dc_ref, ds_ref, prev_ref, out_ref, acc_ref):
    experts, _, feats = dc_ref.shape
    blocks = ds_ref.shape[1]
    qb = feats // blocks
    step = pl.program_id(0)

    @pl.when(step == 0)
    def _():
        acc_ref[...] = prev_ref[...].astype(F32)

    lhs = []
    for e in range(experts):
        other = jnp.where(ids_ref[:, 1:2] == e, theirs_ref[...], jnp.zeros((), BF16))
        lhs.append(jnp.where(ids_ref[:, 0:1] == e, mine_ref[...], other))
    for b in range(blocks):
        cols = slice(b * qb, (b + 1) * qb)
        total = None
        for e in range(experts):
            scaled = lhs[e] * ds_ref[e, b : b + 1, :].astype(BF16)
            part = lax.dot_general(
                scaled, dc_ref[e, :, cols], (((1,), (0,)), ((), ())), preferred_element_type=F32
            )
            total = part if total is None else total + part
        acc_ref[:, cols] += total

    @pl.when(step == pl.num_programs(0) - 1)
    def _():
        out_ref[...] = acc_ref[...].astype(out_ref.dtype)


def down(mine, theirs, ids, dc, ds, prev, first, count, width, out_type):
    experts, _, feats = dc.shape
    blocks, rows = ds.shape[1], mine.shape[0]
    moved = experts * count * width * feats * 2
    h_spec = pl.BlockSpec((rows, width), lambda i: (0, i))
    return pl.pallas_call(
        down_kernel,
        out_shape=jax.ShapeDtypeStruct((rows, feats), out_type),
        grid=(count,),
        in_specs=[
            h_spec,
            h_spec,
            pl.BlockSpec(ids.shape, lambda i: (0, 0)),
            pl.BlockSpec((experts, width, feats), lambda i: (0, first + i, 0)),
            pl.BlockSpec((experts, blocks, width), lambda i: (0, 0, first + i)),
            pl.BlockSpec((rows, feats), lambda i: (0, 0)),
        ],
        out_specs=pl.BlockSpec((rows, feats), lambda i: (0, 0)),
        scratch_shapes=[pltpu.VMEM((rows, feats), F32)],
        cost_estimate=pl.CostEstimate(flops=moved * rows, transcendentals=0, bytes_accessed=moved),
        name="down",
    )(mine, theirs, ids, dc, ds, prev)


def body(fsdp, tp, tokens, route_logits, route_ids, gc, gs, uc, us, dc, ds):
    feats = tokens.shape[1]
    small = jnp.concatenate([route_logits, route_ids.astype(BF16)], axis=1)
    rows = jnp.concatenate([tokens, jnp.pad(small, ((0, 0), (0, 128 - small.shape[1])))], axis=1)
    mask = fsdp // 2
    while mask:
        rows = jnp.concatenate([rows, exchange(rows, "fsdp", mask, fsdp)], axis=0)
        mask //= 2
    x = rows[:, :feats]
    core = lax.axis_index("tp") % 2
    logits = rows[:, feats : feats + 2].astype(F32)
    ids = rows[:, feats + 2 : feats + 4].astype(jnp.int32)
    flip = core == 1
    logits = jnp.where(flip, logits[:, ::-1], logits)
    ids = jnp.where(flip, ids[:, ::-1], ids)
    weight = jax.nn.sigmoid(logits[:, 0:1] - logits[:, 1:2])
    gs, us, ds = (jnp.swapaxes(s, 1, 2) for s in (gs, us, ds))
    units = gc.shape[1]
    width = 256 if units % 256 == 0 else units
    tiles = units // width
    cuts = [0, (tiles + 1) // 2, tiles] if tiles > 1 else [0, tiles]
    spans = [(lo, hi - lo) for lo, hi in zip(cuts[:-1], cuts[1:])]

    hidden = []
    for first, count in spans:
        mine, theirs = gate_up(x, ids, gc, gs, uc, us, first, count, width)
        chip = mine.astype(F32) + exchange(theirs, "tp", 1, tp).astype(F32)
        total, sent, step = chip, chip.astype(BF16), 2
        while step < tp:
            total = total + exchange(sent, "tp", step, tp).astype(F32)
            sent = total.astype(BF16)
            step *= 2
        own = (jax.nn.silu(total[0]) * total[1] * weight).astype(BF16)
        hidden.append((own, exchange(own, "tp", 1, tp)))
    acc = jnp.zeros((x.shape[0], feats), BF16)
    for n, ((first, count), (own, other)) in enumerate(zip(spans, hidden)):
        last = n + 1 == len(spans)
        acc = down(own, other, ids, dc, ds, acc, first, count, width, BF16 if last else F32)
    mask = 1
    while mask < fsdp:
        half = acc.shape[0] // 2
        got = exchange(acc[half:], "fsdp", mask, fsdp)
        acc = (acc[:half].astype(F32) + got.astype(F32)).astype(BF16)
        mask *= 2
    return acc


def solution(mesh):
    fsdp, tp = mesh.shape["fsdp"], mesh.shape["tp"]
    w_spec = P(None, "fsdp", "tp")
    in_specs = (P("fsdp", "tp"), P("fsdp", None), P("fsdp", None)) + (w_spec,) * 6
    return jax.shard_map(
        functools.partial(body, fsdp, tp),
        mesh=mesh,
        in_specs=in_specs,
        out_specs=P("fsdp", "tp"),
        check_vma=False,
    )
```
